32 devices in a mesh: section: 8 (over y, x, core), dp: 4 (over z).
Axes of the slice: x: 2, y: 2, z: 4, core: 2. Of those that a mesh axis runs over, the one named last changes fastest.
Arguments:
- pending_adjoints: bfloat16 [2, 8, 4, 16, 32, 256], P(None, 'section', 'dp'), may hold values from -6 to 6
- objective_adjoints: bfloat16 [3, 4, 16, 32, 256], P(None, 'dp'), may hold values from -6 to 6
- kept_block_entries: bfloat16 [2, 8, 4, 4, 16, 32, 256], P(None, 'section', None, 'dp'), may hold values from -6 to 6
- kept_early_presums: bfloat16 [2, 8, 4, 4, 16, 32, 256], P(None, 'section', None, 'dp'), may hold values from -6 to 6
- kept_later_presums: bfloat16 [2, 8, 4, 4, 16, 32, 256], P(None, 'section', None, 'dp'), may hold values from -6 to 6
- filter_taps: bfloat16 [2, 8, 2, 9, 256, 256], P(None, 'section'), may hold values from -0.1875 to 0.1875
- slot_timetable: int32 [4, 16], replicated, may hold values from 0 to 3, as said below
Outputs:
- final_grads: bfloat16 [2, 8, 4, 16, 32, 256], P(None, 'section', 'dp')
- weight_grads: float32 [2, 8, 2, 9, 256, 256], P(None, 'section', None, None, 'dp')
The draws below stay inside these ranges and needn't reach their ends.
Inputs may be any that keep to these rules, and one draw needn't show every extreme that they name: `slot_timetable`: in each column the slot rises by one from tick to tick, modulo 4, from a starting slot drawn for each section, so each section visits every slot once.
All inputs are finite; a program needn't handle non-finite values.
Results may differ from the reference program's by a relative error of at most 0.017.
Values may be sent and summed in bfloat16 or wider, within the bound.
A program may use at most 192 MiB of HBM per device.

```python
import math
import jax
import jax.numpy as jnp
from jax import lax

FEATURE_PLANES = 256
PICTURE_ROWS = 16
PICTURE_COLUMNS = 32
TICKS = 4
SLOTS = 4
LEVELS = 8
NUMBER_OF_BLOCKS = 16
MICRO_PICTURES = 4
N_SECTION = 8


def draw_slot_timetable(key, part):
    starts = jax.random.randint(jax.random.fold_in(key, 17), (NUMBER_OF_BLOCKS,), 0, SLOTS)
    moments = jnp.arange(TICKS, dtype=jnp.int32)[:, None]
    return ((moments + starts[None, :]) % SLOTS).astype(jnp.int32)


def shard_levels(own_key, extent, split, low, high):
    def one(axis_at, shards_of):
        steps = jax.random.uniform(jax.random.fold_in(jax.random.fold_in(own_key, 6), axis_at), (shards_of,), jnp.float32, low / len(split), high / len(split))
        return jnp.repeat(jnp.exp(steps), extent[axis_at] // shards_of).reshape((-1,) + (1,) * (len(extent) - axis_at - 1))

    factor_of = one(*split[0])
    for cut in split[1:]:
        factor_of = factor_of * one(*cut)
    return factor_of


def normal_values(own_key, shape, width, most, shards=(), kind=jnp.bfloat16):
    result = jax.random.normal(own_key, shape, jnp.float32) * width
    if len(shards) > 0:
        result = shard_levels(own_key, shape, shards, -0.22, 0.18) * result
    return jnp.clip(result, min=-most, max=most).astype(kind)


def setup_inputs(seed: int = 0) -> dict:
    streams_of = jax.random.split(jax.random.key(seed), 8)
    pending_adjoints = normal_values(streams_of[0], (2, LEVELS, MICRO_PICTURES, PICTURE_ROWS, PICTURE_COLUMNS, FEATURE_PLANES), 1.0, 6.0, ((1, 8), (2, 4)))
    objective_adjoints = normal_values(streams_of[1], (TICKS - 1, MICRO_PICTURES, PICTURE_ROWS, PICTURE_COLUMNS, FEATURE_PLANES), 1.0, 6.0, ((1, 4),))
    kept_block_entries = normal_values(streams_of[2], (2, LEVELS, SLOTS, MICRO_PICTURES, PICTURE_ROWS, PICTURE_COLUMNS, FEATURE_PLANES), 1.0, 6.0, ((1, 8), (3, 4)))
    kept_early_presums = normal_values(streams_of[3], (2, LEVELS, SLOTS, MICRO_PICTURES, PICTURE_ROWS, PICTURE_COLUMNS, FEATURE_PLANES), 1.0, 6.0, ((1, 8), (3, 4)))
    kept_later_presums = normal_values(streams_of[4], (2, LEVELS, SLOTS, MICRO_PICTURES, PICTURE_ROWS, PICTURE_COLUMNS, FEATURE_PLANES), 1.0, 6.0, ((1, 8), (3, 4)))
    filter_taps = normal_values(streams_of[5], (2, LEVELS, 2, 9, FEATURE_PLANES, FEATURE_PLANES), (9 * FEATURE_PLANES // 2) ** -0.5, 0.1875, ((1, 8),))
    slot_timetable = draw_slot_timetable(jax.random.fold_in(streams_of[7], 71), 0)
    return dict(pending_adjoints=pending_adjoints, objective_adjoints=objective_adjoints, kept_block_entries=kept_block_entries, kept_early_presums=kept_early_presums, kept_later_presums=kept_later_presums, filter_taps=filter_taps, slot_timetable=slot_timetable)


def patches(field):
    padded = jnp.pad(field, ((0, 0), (1, 1), (1, 1), (0, 0)))
    rows_n = field.shape[1]
    cols_n = field.shape[2]
    views = [padded[:, row_off:row_off + rows_n, col_off:col_off + cols_n, :] for row_off in range(3) for col_off in range(3)]
    return jnp.stack(views, axis=3).reshape(-1, 9 * field.shape[3])

def flipped(kernel):
    return jnp.swapaxes(kernel[::-1], 1, 2).reshape(-1, kernel.shape[2])

def contract_pixels(left, right):
    return lax.dot_general(left, right, (((0,), (0,)), ((), ())), preferred_element_type=jnp.float32)

def section_backward(kernels, inp, pre_one, pre_two, incoming, skipped):
    shape = inp.shape
    chans = shape[3]
    upper_mask = (pre_two > 0).astype(jnp.float32)
    grad_two = ((incoming.astype(jnp.float32) + skipped.astype(jnp.float32)) * upper_mask).astype(jnp.bfloat16)
    activated = jnp.maximum(pre_one, jnp.zeros_like(pre_one))
    wg_two = contract_pixels(patches(activated), grad_two.reshape(-1, chans))
    back_two = jnp.dot(patches(grad_two), flipped(kernels[1]), preferred_element_type=jnp.float32)
    lower_mask = (pre_one > 0).astype(jnp.float32).reshape(-1, chans)
    grad_one = (back_two * lower_mask).astype(jnp.bfloat16)
    wg_one = contract_pixels(patches(inp), grad_one)
    out_grad = jnp.dot(patches(grad_one.reshape(shape)), flipped(kernels[0]), preferred_element_type=jnp.float32)
    out_grad = out_grad.astype(jnp.bfloat16).reshape(shape)
    return (out_grad, jnp.stack([wg_one, wg_two]).reshape(2, 9, chans, chans))

def flat_sections(array):
    return array.reshape((array.shape[0] * array.shape[1],) + array.shape[2:])

def reference(pending_adjoints, objective_adjoints, kept_block_entries, kept_early_presums, kept_later_presums, filter_taps, slot_timetable):
    levels = N_SECTION
    adjoint_propagate = flat_sections(pending_adjoints)
    bypass_connections = jnp.zeros_like(adjoint_propagate)
    taps_flat = flat_sections(filter_taps)
    entries_flat = flat_sections(kept_block_entries)
    early_flat = flat_sections(kept_early_presums)
    later_flat = flat_sections(kept_later_presums)
    total = jnp.zeros(taps_flat.shape, jnp.float32)
    for moment in range(TICKS):

        def per_section(items):
            kernels, inputs_all, pre_all, post_all, incoming, skipped, slot_index = items
            inp = lax.dynamic_index_in_dim(inputs_all, slot_index, 0, keepdims=False)
            pre_one = lax.dynamic_index_in_dim(pre_all, slot_index, 0, keepdims=False)
            pre_two = lax.dynamic_index_in_dim(post_all, slot_index, 0, keepdims=False)
            return section_backward(kernels, inp, pre_one, pre_two, incoming, skipped)
        out_grad, wgrad = lax.map(per_section, (taps_flat, entries_flat, early_flat, later_flat, adjoint_propagate, bypass_connections, slot_timetable[moment].astype(jnp.int32)))
        total = total + wgrad
        if moment < TICKS - 1:
            enc_out = out_grad[:levels]
            dec_out = out_grad[levels:]
            enc_next = jnp.concatenate([enc_out[1:], dec_out[levels - 1:levels]], axis=0)
            dec_next = jnp.concatenate([objective_adjoints[moment][None], dec_out[:levels - 1]], axis=0)
            adjoint_propagate = jnp.concatenate([enc_next, dec_next], axis=0)
            enc_skip = jnp.concatenate([dec_out[:levels - 1], jnp.zeros_like(dec_out[:1])], axis=0)
            bypass_connections = jnp.concatenate([enc_skip, jnp.zeros_like(dec_out)], axis=0)
    scale = 1.0 / math.sqrt(TICKS * MICRO_PICTURES * PICTURE_ROWS * PICTURE_COLUMNS)
    final_grads = out_grad.reshape(pending_adjoints.shape)
    weight_grads = (total * scale).reshape(filter_taps.shape)
    return (final_grads, weight_grads)
```

```python
import functools
import math

import jax
import jax.numpy as jnp
from jax import lax
from jax.experimental import pallas as pl
from jax.experimental.pallas import tpu as pltpu
from jax.sharding import PartitionSpec as P

MESH = pl.DeviceIdType.MESH
LAG = 3


def kernel(
    dims,
    slots,
    pend,
    obj,
    ent,
    pre1,
    pre2,
    taps,
    fin,
    wout,
    cur,
    outg,
    shf,
    act_t,
    own,
    buf_r,
    buf_l,
    enc_s,
    enc_r,
    dec_s,
    dec_r,
    rs,
    rr,
    ls,
    lr,
):
    ticks, levels, replicas, rows, cols, chans, scale = dims
    pix = rows * cols
    share = chans // replicas
    level = lax.axis_index("section")
    rep = lax.axis_index("dp")
    f32, bf16 = jnp.float32, jnp.bfloat16
    has_up, has_down = level < levels - 1, level > 0
    has_right, has_left = rep < replicas - 1, rep > 0

    def hop(src, dst, send, recv, axis, step):
        here = {"section": level, "dp": rep}
        here[axis] = here[axis] + step
        return pltpu.make_async_remote_copy(
            src_ref=src,
            dst_ref=dst,
            send_sem=send,
            recv_sem=recv,
            device_id=(here["section"], here["dp"]),
            device_id_type=MESH,
        )

    barrier = pltpu.get_barrier_semaphore()
    around = (
        (has_up, level + 1, rep),
        (has_down, level - 1, rep),
        (has_right, level, rep + 1),
        (has_left, level, rep - 1),
    )
    for exists, a, b in around:

        @pl.when(exists)
        def _(a=a, b=b):
            pl.semaphore_signal(barrier, inc=1, device_id=(a, b), device_id_type=MESH)

    peers = sum(exists.astype(jnp.int32) for exists, _a, _b in around)
    pl.semaphore_wait(barrier, peers)

    edge = jnp.zeros((cols, chans), bf16)

    def clear(i, carry):
        for h in range(2):
            for c in range(2):
                for d in range(3):
                    shf[h, c, i, d, 0:cols, :] = edge
                    shf[h, c, i, d, cols + pix : 2 * cols + pix, :] = edge
        return carry

    lax.fori_loop(0, ticks, clear, 0)
    column = lax.broadcasted_iota(jnp.int32, (pix, chans), 0) % cols

    def keep(h, c, t, grad):
        wide = grad.astype(f32)
        left = jnp.where(column == 0, 0.0, pltpu.roll(wide, 1, 0))
        right = jnp.where(column == cols - 1, 0.0, pltpu.roll(wide, pix - 1, 0))
        shf[h, c, t, 0, cols : cols + pix, :] = left.astype(bf16)
        shf[h, c, t, 1, cols : cols + pix, :] = grad
        shf[h, c, t, 2, cols : cols + pix, :] = right.astype(bf16)

    def convolve(h, c, t):
        total = None
        for k in range(9):
            piece = lax.dot_general(
                shf[h, c, t, k % 3, (k // 3) * cols : (k // 3) * cols + pix, :],
                taps[h, c, 8 - k],
                (((1,), (1,)), ((), ())),
                preferred_element_type=f32,
            )
            total = piece if total is None else total + piece
        return total

    def slot_of(t, h):
        return slots[t, h * levels + level]

    def upper(h, t, first_tick):
        if first_tick:
            flow = pend[h].astype(f32)
        elif h == 0:
            arrived = cur[t, 0].astype(f32)
            flow = outg[t - 1, 1].astype(f32) + jnp.where(has_up, arrived, 0.0)
        else:
            flow = jnp.where(has_down, cur[t, 1], obj[t - 1]).astype(f32)
        later = pre2[h, slot_of(t, h)].astype(f32)
        keep(h, 1, t, jnp.where(later > 0, flow, 0.0).astype(bf16))

    def lower(h, t):
        early = pre1[h, slot_of(t, h)].astype(f32)
        keep(h, 0, t, jnp.where(early > 0, convolve(h, 1, t), 0.0).astype(bf16))
        outg[t, h] = convolve(h, 0, t).astype(bf16)

    def enc_hop(t):
        return hop(outg.at[t, 0], cur.at[t + 1, 0], enc_s.at[t], enc_r.at[t], "section", -1)

    def dec_hop(t):
        return hop(outg.at[t, 1], cur.at[t + 1, 1], dec_s.at[t], dec_r.at[t], "section", 1)

    def send(t):
        @pl.when(has_up)
        def _():
            dec_hop(t).start()

    def send_enc(t):
        @pl.when(has_down)
        def _():
            enc_hop(t).start()

    def arrive_dec(t):
        @pl.when(has_down)
        def _():
            dec_hop(t - 1).wait_recv()

    def arrive_enc(t):
        @pl.when(has_up)
        def _():
            enc_hop(t - 1).wait_recv()

    def turn(t):
        for h in range(2):
            place = pl.ds(pl.multiple_of(t * pix, pix), pix)
            act_t[h, 0, :, place] = ent[h, slot_of(t, h)].T
            early = pre1[h, slot_of(t, h)]
            act_t[h, 1, :, place] = jnp.maximum(early, jnp.zeros_like(early)).T

    upper(1, 0, True)
    lower(1, 0)
    send(0)
    upper(0, 0, True)
    lower(0, 0)
    send_enc(0)
    turn(0)

    def tick(t, carry):
        arrive_dec(t)
        upper(1, t, False)
        lower(1, t)
        send(t)
        arrive_enc(t)
        upper(0, t, False)
        lower(0, t)
        send_enc(t)
        turn(t)
        return carry

    lax.fori_loop(1, ticks - 1, tick, 0)
    final = ticks - 1
    turn(final)
    arrive_dec(final)
    upper(1, final, False)
    arrive_enc(final)
    upper(0, final, False)

    def right_hop(u, j):
        return hop(buf_r.at[u, j], buf_r.at[u, j], rs.at[u, j], rr.at[u, j], "dp", 1)

    def left_hop(u, j):
        return hop(buf_l.at[u, j], buf_l.at[u, j], ls.at[u, j], lr.at[u, j], "dp", -1)

    def unit(c, u):
        h, a = (u % 6) // 3, u % 3
        start = pl.multiple_of((2 - a) * cols, cols)
        left = act_t[h, c]
        for i in range(3):
            right = jnp.concatenate(
                [shf[h, c, t, 2 - i, pl.ds(start, pix), :] for t in range(ticks)], axis=0
            )
            own[u % (LAG + 1), :, i * chans : (i + 1) * chans] = jnp.dot(
                left, right, preferred_element_type=f32
            )

    def mine(u, j):
        return own[u % (LAG + 1), j * share : (j + 1) * share, :]

    def lead(u):
        for j in reversed(range(1, replicas)):

            @pl.when(rep == 0)
            def _(j=j):
                buf_r[u, j] = mine(u, j).astype(bf16)
                right_hop(u, j).start()

        for j in range(replicas - 1):

            @pl.when(rep == replicas - 1)
            def _(j=j):
                buf_l[u, j] = mine(u, j).astype(bf16)
                left_hop(u, j).start()

    def relay(u):
        for j in reversed(range(1, replicas)):

            @pl.when(has_left & (rep < j))
            def _(j=j):
                right_hop(u, j).wait_recv()
                buf_r[u, j] = (mine(u, j) + buf_r[u, j].astype(f32)).astype(bf16)
                right_hop(u, j).start()

        for j in range(replicas - 1):

            @pl.when(has_right & (rep > j))
            def _(j=j):
                left_hop(u, j).wait_recv()
                buf_l[u, j] = (mine(u, j) + buf_l[u, j].astype(f32)).astype(bf16)
                left_hop(u, j).start()

        c, h, a = 1 - u // 6, (u % 6) // 3, u % 3
        for j in range(replicas):

            @pl.when(rep == j)
            def _(j=j):
                total = mine(u, j)
                if j > 0:
                    right_hop(u, j).wait_recv()
                    total = total + buf_r[u, j].astype(f32)
                if j < replicas - 1:
                    left_hop(u, j).wait_recv()
                    total = total + buf_l[u, j].astype(f32)
                total = total * scale
                for i in range(3):
                    wout[h, c, a * 3 + i] = total[:, i * chans : (i + 1) * chans]

    def first_half(u, carry):
        unit(1, u)
        lead(u)

        @pl.when(u >= LAG)
        def _():
            relay(u - LAG)

        return carry

    lax.fori_loop(0, 6, first_half, 0)
    for h in range(2):
        lower(h, final)
        fin[h] = outg[final, h]

    def second_half(u, carry):
        unit(0, u)
        lead(u)
        relay(u - LAG)
        return carry

    lax.fori_loop(6, 12, second_half, 0)

    def rest(u, carry):
        relay(u)
        return carry

    lax.fori_loop(12 - LAG, 12, rest, 0)

    def drain(u, carry):
        for j in range(replicas):

            @pl.when(rep < j)
            def _(j=j):
                right_hop(u, j).wait_send()

            @pl.when(rep > j)
            def _(j=j):
                left_hop(u, j).wait_send()

        return carry

    lax.fori_loop(0, 12, drain, 0)

    def drain_chain(t, carry):
        @pl.when(has_up)
        def _():
            dec_hop(t).wait_send()

        @pl.when(has_down)
        def _():
            enc_hop(t).wait_send()

        return carry

    lax.fori_loop(0, ticks - 1, drain_chain, 0)


def on_device(pending, objective, entries, early, later, taps, slots):
    levels = lax.axis_size("section")
    replicas = lax.axis_size("dp")
    images, rows, cols, chans = pending.shape[2:]
    ticks = slots.shape[0]
    kept = entries.shape[2]
    pix = images * rows * cols
    scale = 1.0 / math.sqrt(ticks * replicas * pix)
    dims = (ticks, levels, replicas, rows, cols, chans, scale)
    bf16 = jnp.bfloat16
    share = chans // replicas
    whole = pl.BlockSpec(memory_space=pltpu.VMEM)
    dma = pltpu.SemaphoreType.DMA
    fin, wout = pl.pallas_call(
        functools.partial(kernel, dims),
        out_shape=(
            jax.ShapeDtypeStruct((2, pix, chans), bf16),
            jax.ShapeDtypeStruct((2, 2, 9, share, chans), jnp.float32),
        ),
        in_specs=[pl.BlockSpec(memory_space=pltpu.SMEM)] + [whole] * 6,
        out_specs=(whole, whole),
        scratch_shapes=[
            pltpu.VMEM((ticks, 2, pix, chans), bf16),
            pltpu.VMEM((ticks, 2, pix, chans), bf16),
            pltpu.VMEM((2, 2, ticks, 3, pix + 2 * cols, chans), bf16),
            pltpu.VMEM((2, 2, chans, ticks * pix), bf16),
            pltpu.VMEM((LAG + 1, chans, 3 * chans), jnp.float32),
            pltpu.VMEM((12, replicas, share, 3 * chans), bf16),
            pltpu.VMEM((12, replicas, share, 3 * chans), bf16),
            dma((ticks - 1,)),
            dma((ticks - 1,)),
            dma((ticks - 1,)),
            dma((ticks - 1,)),
            dma((12, replicas)),
            dma((12, replicas)),
            dma((12, replicas)),
            dma((12, replicas)),
        ],
        compiler_params=pltpu.CompilerParams(
            collective_id=0, has_side_effects=True, vmem_limit_bytes=67043328
        ),
    )(
        slots,
        pending.reshape(2, pix, chans),
        objective.reshape(-1, pix, chans),
        entries.reshape(2, kept, pix, chans),
        early.reshape(2, kept, pix, chans),
        later.reshape(2, kept, pix, chans),
        taps.reshape(2, 2, 9, chans, chans),
    )
    return (
        fin.reshape(2, 1, images, rows, cols, chans),
        wout.reshape(2, 1, 2, 9, share, chans),
    )


def solution(mesh):
    placed = (
        P(None, "section", "dp", None, None, None),
        P(None, "dp", None, None, None),
        P(None, "section", None, "dp", None, None, None),
        P(None, "section", None, "dp", None, None, None),
        P(None, "section", None, "dp", None, None, None),
        P(None, "section", None, None, None, None),
        P(),
    )
    return jax.shard_map(
        on_device,
        mesh=mesh,
        in_specs=placed,
        out_specs=(
            P(None, "section", "dp", None, None, None),
            P(None, "section", None, None, "dp", None),
        ),
        check_vma=False,
    )
```

```python
import functools
import math

import jax
import jax.numpy as jnp
from jax import lax
from jax.experimental import pallas as pl
from jax.experimental.pallas import tpu as pltpu
from jax.sharding import PartitionSpec as P

MESH = pl.DeviceIdType.MESH
LAG = 3


def kernel(
    dims,
    slots,
    pend,
    obj,
    pre1,
    pre2,
    ent_in,
    taps_in,
    fin,
    wout,
    ent,
    taps,
    loaded,
    cur,
    outg,
    shf,
    act_t,
    own,
    buf_r,
    buf_l,
    enc_s,
    enc_r,
    dec_s,
    dec_r,
    rs,
    rr,
    ls,
    lr,
):
    ticks, levels, replicas, rows, cols, chans, scale = dims
    pix = rows * cols
    share = chans // replicas
    level = lax.axis_index("section")
    rep = lax.axis_index("dp")
    f32, bf16 = jnp.float32, jnp.bfloat16
    has_up, has_down = level < levels - 1, level > 0
    has_right, has_left = rep < replicas - 1, rep > 0

    def hop(src, dst, send, recv, axis, step):
        here = {"section": level, "dp": rep}
        here[axis] = here[axis] + step
        return pltpu.make_async_remote_copy(
            src_ref=src,
            dst_ref=dst,
            send_sem=send,
            recv_sem=recv,
            device_id=(here["section"], here["dp"]),
            device_id_type=MESH,
        )

    def fetch(h, c):
        return pltpu.make_async_copy(taps_in.at[h, c], taps.at[h, c], loaded.at[h, c])

    def fetch_entries():
        return pltpu.make_async_copy(ent_in, ent, loaded.at[2, 0])

    fetch(1, 1).start()
    fetch(1, 0).start()
    fetch(0, 1).start()
    fetch(0, 0).start()
    fetch_entries().start()

    barrier = pltpu.get_barrier_semaphore()
    around = (
        (has_up, level + 1, rep),
        (has_down, level - 1, rep),
        (has_right, level, rep + 1),
        (has_left, level, rep - 1),
    )
    for exists, a, b in around:

        @pl.when(exists)
        def _(a=a, b=b):
            pl.semaphore_signal(barrier, inc=1, device_id=(a, b), device_id_type=MESH)

    peers = sum(exists.astype(jnp.int32) for exists, _a, _b in around)
    pl.semaphore_wait(barrier, peers)

    edge = jnp.zeros((cols, chans), bf16)

    def clear(i, carry):
        for h in range(2):
            for c in range(2):
                for d in range(3):
                    shf[h, c, i, d, 0:cols, :] = edge
                    shf[h, c, i, d, cols + pix : 2 * cols + pix, :] = edge
        return carry

    lax.fori_loop(0, ticks, clear, 0)
    column = lax.broadcasted_iota(jnp.int32, (pix, chans), 0) % cols

    def keep(h, c, t, grad):
        wide = grad.astype(f32)
        left = jnp.where(column == 0, 0.0, pltpu.roll(wide, 1, 0))
        right = jnp.where(column == cols - 1, 0.0, pltpu.roll(wide, pix - 1, 0))
        shf[h, c, t, 0, cols : cols + pix, :] = left.astype(bf16)
        shf[h, c, t, 1, cols : cols + pix, :] = grad
        shf[h, c, t, 2, cols : cols + pix, :] = right.astype(bf16)

    def convolve(h, c, t):
        wide = jnp.concatenate(
            [
                shf[h, c, t, k % 3, (k // 3) * cols : (k // 3) * cols + pix, :]
                for k in range(9)
            ],
            axis=1,
        )
        filt = jnp.concatenate([taps[h, c, 8 - k] for k in range(9)], axis=1)
        return lax.dot_general(
            wide, filt, (((1,), (1,)), ((), ())), preferred_element_type=f32
        )

    def slot_of(t, h):
        return slots[t, h * levels + level]

    def upper(h, t, first_tick):
        if first_tick:
            flow = pend[h].astype(f32)
        elif h == 0:
            arrived = cur[t, 0].astype(f32)
            flow = outg[t - 1, 1].astype(f32) + jnp.where(has_up, arrived, 0.0)
        else:
            flow = jnp.where(has_down, cur[t, 1], obj[t - 1]).astype(f32)
        later = pre2[h, slot_of(t, h)].astype(f32)
        keep(h, 1, t, jnp.where(later > 0, flow, 0.0).astype(bf16))

    def lower(h, t):
        early = pre1[h, slot_of(t, h)].astype(f32)
        keep(h, 0, t, jnp.where(early > 0, convolve(h, 1, t), 0.0).astype(bf16))
        outg[t, h] = convolve(h, 0, t).astype(bf16)

    def enc_hop(t):
        return hop(outg.at[t, 0], cur.at[t + 1, 0], enc_s.at[t], enc_r.at[t], "section", -1)

    def dec_hop(t):
        return hop(outg.at[t, 1], cur.at[t + 1, 1], dec_s.at[t], dec_r.at[t], "section", 1)

    def send(t):
        @pl.when(has_up)
        def _():
            dec_hop(t).start()

    def send_enc(t):
        @pl.when(has_down)
        def _():
            enc_hop(t).start()

    def arrive_dec(t):
        @pl.when(has_down)
        def _():
            dec_hop(t - 1).wait_recv()

    def arrive_enc(t):
        @pl.when(has_up)
        def _():
            enc_hop(t - 1).wait_recv()

    def turn(h, c, t):
        place = pl.ds(pl.multiple_of(t * pix, pix), pix)
        if c == 0:
            act_t[h, 0, :, place] = ent[h, slot_of(t, h)].T
        else:
            early = pre1[h, slot_of(t, h)]
            act_t[h, 1, :, place] = jnp.maximum(early, jnp.zeros_like(early)).T

    def turn_all(h, c):
        def one(t, carry):
            turn(h, c, t)
            return carry

        lax.fori_loop(0, ticks, one, 0)

    upper(1, 0, True)
    fetch(1, 1).wait()
    fetch(1, 0).wait()
    lower(1, 0)
    send(0)
    upper(0, 0, True)
    fetch(0, 1).wait()
    fetch(0, 0).wait()
    lower(0, 0)
    send_enc(0)
    turn(1, 1, 0)

    def tick(t, carry):
        arrive_dec(t)
        upper(1, t, False)
        lower(1, t)
        send(t)
        arrive_enc(t)
        upper(0, t, False)
        lower(0, t)
        send_enc(t)
        turn(1, 1, t)
        return carry

    lax.fori_loop(1, ticks - 1, tick, 0)
    final = ticks - 1
    turn(1, 1, final)
    arrive_dec(final)
    upper(1, final, False)

    def right_hop(u, j):
        return hop(buf_r.at[u, j], buf_r.at[u, j], rs.at[u, j], rr.at[u, j], "dp", 1)

    def left_hop(u, j):
        return hop(buf_l.at[u, j], buf_l.at[u, j], ls.at[u, j], lr.at[u, j], "dp", -1)

    def unit(h, c, u):
        a = u % 3
        start = pl.multiple_of((2 - a) * cols, cols)
        left = act_t[h, c]
        for i in range(3):
            right = jnp.concatenate(
                [shf[h, c, t, 2 - i, pl.ds(start, pix), :] for t in range(ticks)], axis=0
            )
            own[u % (LAG + 2), :, i * chans : (i + 1) * chans] = jnp.dot(
                left, right, preferred_element_type=f32
            )

    def mine(u, j):
        return own[u % (LAG + 2), j * share : (j + 1) * share, :]

    def lead(u):
        for j in reversed(range(1, replicas)):

            @pl.when(rep == 0)
            def _(j=j):
                buf_r[u, j] = mine(u, j).astype(bf16)
                right_hop(u, j).start()

        for j in range(replicas - 1):

            @pl.when(rep == replicas - 1)
            def _(j=j):
                buf_l[u, j] = mine(u, j).astype(bf16)
                left_hop(u, j).start()

    def relay_right(u):
        for j in reversed(range(1, replicas)):

            @pl.when(has_left & (rep < j))
            def _(j=j):
                right_hop(u, j).wait_recv()
                buf_r[u, j] = (mine(u, j) + buf_r[u, j].astype(f32)).astype(bf16)
                right_hop(u, j).start()

    def relay_left(u):
        for j in range(replicas - 1):

            @pl.when(has_right & (rep > j))
            def _(j=j):
                left_hop(u, j).wait_recv()
                buf_l[u, j] = (mine(u, j) + buf_l[u, j].astype(f32)).astype(bf16)
                left_hop(u, j).start()

    near_left = rep * 2 < replicas

    def relay_near(u):
        @pl.when(near_left)
        def _():
            relay_right(u)

        @pl.when(jnp.logical_not(near_left))
        def _():
            relay_left(u)

    def relay_far(u):
        @pl.when(near_left)
        def _():
            relay_left(u)

        @pl.when(jnp.logical_not(near_left))
        def _():
            relay_right(u)

    def finish(u):
        c, h, a = 1 - u // 6, 1 - (u // 3) % 2, u % 3
        for j in range(replicas):

            @pl.when(rep == j)
            def _(j=j):
                total = mine(u, j)
                if j > 0:
                    right_hop(u, j).wait_recv()
                    total = total + buf_r[u, j].astype(f32)
                if j < replicas - 1:
                    left_hop(u, j).wait_recv()
                    total = total + buf_l[u, j].astype(f32)
                total = total * scale
                for i in range(3):
                    wout[h, c, a * 3 + i] = total[:, i * chans : (i + 1) * chans]

    def advance(u):
        @pl.when((u >= LAG) & (u < 12 + LAG))
        def _():
            relay_near(u - LAG)

        @pl.when(u > LAG)
        def _():
            relay_far(u - LAG - 1)
            finish(u - LAG - 1)

    def group(g):
        def one(u, carry):
            unit(1 - g % 2, 1 - g // 2, u)
            lead(u)
            advance(u)
            return carry

        lax.fori_loop(3 * g, 3 * g + 3, one, 0)

    group(0)
    turn_all(0, 1)
    fetch_entries().wait()
    arrive_enc(final)
    upper(0, final, False)
    group(1)
    turn_all(1, 0)
    lower(1, final)
    fin[1] = outg[final, 1]
    group(2)
    turn_all(0, 0)
    lower(0, final)
    fin[0] = outg[final, 0]
    group(3)

    def rest(u, carry):
        advance(u)
        return carry

    lax.fori_loop(12, 13 + LAG, rest, 0)

    def drain(u, carry):
        for j in range(replicas):

            @pl.when(rep < j)
            def _(j=j):
                right_hop(u, j).wait_send()

            @pl.when(rep > j)
            def _(j=j):
                left_hop(u, j).wait_send()

        return carry

    lax.fori_loop(0, 12, drain, 0)

    def drain_chain(t, carry):
        @pl.when(has_up)
        def _():
            dec_hop(t).wait_send()

        @pl.when(has_down)
        def _():
            enc_hop(t).wait_send()

        return carry

    lax.fori_loop(0, ticks - 1, drain_chain, 0)


def on_device(pending, objective, entries, early, later, taps, slots):
    levels = lax.axis_size("section")
    replicas = lax.axis_size("dp")
    images, rows, cols, chans = pending.shape[2:]
    ticks = slots.shape[0]
    kept = entries.shape[2]
    pix = images * rows * cols
    scale = 1.0 / math.sqrt(ticks * replicas * pix)
    dims = (ticks, levels, replicas, rows, cols, chans, scale)
    bf16 = jnp.bfloat16
    share = chans // replicas
    whole = pl.BlockSpec(memory_space=pltpu.VMEM)
    anywhere = pl.BlockSpec(memory_space=pl.ANY)
    dma = pltpu.SemaphoreType.DMA
    fin, wout = pl.pallas_call(
        functools.partial(kernel, dims),
        out_shape=(
            jax.ShapeDtypeStruct((2, pix, chans), bf16),
            jax.ShapeDtypeStruct((2, 2, 9, share, chans), jnp.float32),
        ),
        in_specs=[pl.BlockSpec(memory_space=pltpu.SMEM)] + [whole] * 4 + [anywhere] * 2,
        out_specs=(whole, whole),
        scratch_shapes=[
            pltpu.VMEM((2, kept, pix, chans), bf16),
            pltpu.VMEM((2, 2, 9, chans, chans), bf16),
            dma((3, 2)),
            pltpu.VMEM((ticks, 2, pix, chans), bf16),
            pltpu.VMEM((ticks, 2, pix, chans), bf16),
            pltpu.VMEM((2, 2, ticks, 3, pix + 2 * cols, chans), bf16),
            pltpu.VMEM((2, 2, chans, ticks * pix), bf16),
            pltpu.VMEM((LAG + 2, chans, 3 * chans), jnp.float32),
            pltpu.VMEM((12, replicas, share, 3 * chans), bf16),
            pltpu.VMEM((12, replicas, share, 3 * chans), bf16),
            dma((ticks - 1,)),
            dma((ticks - 1,)),
            dma((ticks - 1,)),
            dma((ticks - 1,)),
            dma((12, replicas)),
            dma((12, replicas)),
            dma((12, replicas)),
            dma((12, replicas)),
        ],
        compiler_params=pltpu.CompilerParams(
            collective_id=0, has_side_effects=True, vmem_limit_bytes=67043328
        ),
    )(
        slots,
        pending.reshape(2, pix, chans),
        objective.reshape(-1, pix, chans),
        early.reshape(2, kept, pix, chans),
        later.reshape(2, kept, pix, chans),
        entries.reshape(2, kept, pix, chans),
        taps.reshape(2, 2, 9, chans, chans),
    )
    return (
        fin.reshape(2, 1, images, rows, cols, chans),
        wout.reshape(2, 1, 2, 9, share, chans),
    )


def solution(mesh):
    placed = (
        P(None, "section", "dp", None, None, None),
        P(None, "dp", None, None, None),
        P(None, "section", None, "dp", None, None, None),
        P(None, "section", None, "dp", None, None, None),
        P(None, "section", None, "dp", None, None, None),
        P(None, "section", None, None, None, None),
        P(),
    )
    return jax.shard_map(
        on_device,
        mesh=mesh,
        in_specs=placed,
        out_specs=(
            P(None, "section", "dp", None, None, None),
            P(None, "section", None, None, "dp", None),
        ),
        check_vma=False,
    )
```

```python
import functools
import math

import jax
import jax.numpy as jnp
from jax import lax
from jax.experimental import pallas as pl
from jax.experimental.pallas import tpu as pltpu
from jax.sharding import PartitionSpec as P

MESH = pl.DeviceIdType.MESH
LAG = 3


def kernel(
    dims,
    slots,
    pend,
    pre2,
    obj_in,
    pre1_in,
    ent_in,
    taps_in,
    fin,
    wout,
    obj,
    pre1,
    ent,
    taps,
    loaded,
    cur,
    outg,
    shf,
    act_t,
    own,
    buf_r,
    buf_l,
    enc_s,
    enc_r,
    dec_s,
    dec_r,
    rs,
    rr,
    ls,
    lr,
):
    ticks, levels, replicas, rows, cols, chans = dims
    pix = rows * cols
    share = chans // replicas
    level = lax.axis_index("section")
    rep = lax.axis_index("dp")
    f32, bf16 = jnp.float32, jnp.bfloat16
    has_up, has_down = level < levels - 1, level > 0
    has_right, has_left = rep < replicas - 1, rep > 0

    def hop(src, dst, send, recv, axis, step):
        here = {"section": level, "dp": rep}
        here[axis] = here[axis] + step
        return pltpu.make_async_remote_copy(
            src_ref=src,
            dst_ref=dst,
            send_sem=send,
            recv_sem=recv,
            device_id=(here["section"], here["dp"]),
            device_id_type=MESH,
        )

    def fetch(h, c):
        return pltpu.make_async_copy(taps_in.at[h, c], taps.at[h, c], loaded.at[h, c])

    def fetch_early():
        return pltpu.make_async_copy(pre1_in, pre1, loaded.at[2, 1])

    def fetch_objective():
        return pltpu.make_async_copy(obj_in, obj, loaded.at[3, 0])

    def fetch_entries():
        return pltpu.make_async_copy(ent_in, ent, loaded.at[2, 0])

    fetch(1, 1).start()
    fetch_early().start()
    fetch(1, 0).start()
    fetch(0, 1).start()
    fetch(0, 0).start()
    fetch_objective().start()
    fetch_entries().start()

    barrier = pltpu.get_barrier_semaphore()
    around = (
        (has_up, level + 1, rep),
        (has_down, level - 1, rep),
        (has_right, level, rep + 1),
        (has_left, level, rep - 1),
    )
    for exists, a, b in around:

        @pl.when(exists)
        def _(a=a, b=b):
            pl.semaphore_signal(barrier, inc=1, device_id=(a, b), device_id_type=MESH)

    peers = sum(exists.astype(jnp.int32) for exists, _a, _b in around)

    edge = jnp.zeros((cols, chans), bf16)

    def clear(i, carry):
        for h in range(2):
            for c in range(2):
                for d in range(3):
                    shf[h, c, i, d, 0:cols, :] = edge
                    shf[h, c, i, d, cols + pix : 2 * cols + pix, :] = edge
        return carry

    lax.fori_loop(0, ticks, clear, 0)
    column = lax.broadcasted_iota(jnp.int32, (pix, chans), 0) % cols

    def keep(h, c, t, grad):
        wide = grad.astype(f32)
        left = jnp.where(column == 0, 0.0, pltpu.roll(wide, 1, 0))
        right = jnp.where(column == cols - 1, 0.0, pltpu.roll(wide, pix - 1, 0))
        shf[h, c, t, 0, cols : cols + pix, :] = left.astype(bf16)
        shf[h, c, t, 1, cols : cols + pix, :] = grad
        shf[h, c, t, 2, cols : cols + pix, :] = right.astype(bf16)

    def convolve(h, c, t):
        filt = jnp.concatenate([taps[h, c, 8 - k] for k in range(9)], axis=1)
        half = pix // 2
        parts = []
        for lo in (0, half):
            wide = jnp.concatenate(
                [
                    shf[h, c, t, k % 3, (k // 3) * cols + lo : (k // 3) * cols + lo + half, :]
                    for k in range(9)
                ],
                axis=1,
            )
            parts.append(
                lax.dot_general(
                    wide, filt, (((1,), (1,)), ((), ())), preferred_element_type=f32
                )
            )
        return jnp.concatenate(parts, axis=0)

    def slot_of(t, h):
        return slots[t, h * levels + level]

    def upper(h, t, first_tick):
        if first_tick:
            flow = pend[h].astype(f32)
        elif h == 0:
            arrived = cur[t, 0].astype(f32)
            flow = outg[t - 1, 1].astype(f32) + jnp.where(has_up, arrived, 0.0)
        else:
            flow = jnp.where(has_down, cur[t, 1], obj[t - 1]).astype(f32)
        later = pre2[h, slot_of(t, h)].astype(f32)
        keep(h, 1, t, jnp.where(later > 0, flow, 0.0).astype(bf16))

    def lower(h, t):
        early = pre1[h, slot_of(t, h)].astype(f32)
        keep(h, 0, t, jnp.where(early > 0, convolve(h, 1, t), 0.0).astype(bf16))
        outg[t, h] = convolve(h, 0, t).astype(bf16)

    def enc_hop(t):
        return hop(outg.at[t, 0], cur.at[t + 1, 0], enc_s.at[t], enc_r.at[t], "section", -1)

    def dec_hop(t):
        return hop(outg.at[t, 1], cur.at[t + 1, 1], dec_s.at[t], dec_r.at[t], "section", 1)

    def send(t):
        @pl.when(has_up)
        def _():
            dec_hop(t).start()

    def send_enc(t):
        @pl.when(has_down)
        def _():
            enc_hop(t).start()

    def arrive_dec(t):
        @pl.when(has_down)
        def _():
            dec_hop(t - 1).wait_recv()

    def arrive_enc(t):
        @pl.when(has_up)
        def _():
            enc_hop(t - 1).wait_recv()

    def turn(h, c, t):
        place = pl.ds(pl.multiple_of(t * pix, pix), pix)
        if c == 0:
            act_t[h, 0, :, place] = ent[h, slot_of(t, h)].T
        else:
            early = pre1[h, slot_of(t, h)]
            act_t[h, 1, :, place] = jnp.maximum(early, jnp.zeros_like(early)).T

    def turn_all(h, c):
        def one(t, carry):
            turn(h, c, t)
            return carry

        lax.fori_loop(0, ticks, one, 0)

    upper(1, 0, True)
    fetch(1, 1).wait()
    fetch_early().wait()
    fetch(1, 0).wait()
    lower(1, 0)
    pl.semaphore_wait(barrier, peers)
    send(0)
    upper(0, 0, True)
    fetch(0, 1).wait()
    fetch(0, 0).wait()
    lower(0, 0)
    send_enc(0)
    turn(1, 1, 0)

    fetch_objective().wait()

    def tick(t, carry):
        arrive_dec(t)
        upper(1, t, False)
        lower(1, t)
        send(t)
        arrive_enc(t)
        upper(0, t, False)
        lower(0, t)
        send_enc(t)
        turn(1, 1, t)
        return carry

    lax.fori_loop(1, ticks - 1, tick, 0)
    final = ticks - 1
    turn(1, 1, final)
    arrive_dec(final)
    upper(1, final, False)

    def right_hop(u, j):
        return hop(buf_r.at[u, j], buf_r.at[u, j], rs.at[u, j], rr.at[u, j], "dp", 1)

    def left_hop(u, j):
        return hop(buf_l.at[u, j], buf_l.at[u, j], ls.at[u, j], lr.at[u, j], "dp", -1)

    def unit(h, c, u):
        a = u % 3
        start = pl.multiple_of((2 - a) * cols, cols)
        left = act_t[h, c]
        for i in range(3):
            right = jnp.concatenate(
                [shf[h, c, t, 2 - i, pl.ds(start, pix), :] for t in range(ticks)], axis=0
            )
            own[u % (LAG + 2), :, i * chans : (i + 1) * chans] = jnp.dot(
                left, right, preferred_element_type=f32
            )

    def mine(u, j):
        return own[u % (LAG + 2), j * share : (j + 1) * share, :]

    def lead(u):
        for j in reversed(range(1, replicas)):

            @pl.when(rep == 0)
            def _(j=j):
                buf_r[u, j] = mine(u, j).astype(bf16)
                right_hop(u, j).start()

        for j in range(replicas - 1):

            @pl.when(rep == replicas - 1)
            def _(j=j):
                buf_l[u, j] = mine(u, j).astype(bf16)
                left_hop(u, j).start()

    def relay_right(u):
        for j in reversed(range(1, replicas)):

            @pl.when(has_left & (rep < j))
            def _(j=j):
                right_hop(u, j).wait_recv()
                buf_r[u, j] = (mine(u, j) + buf_r[u, j].astype(f32)).astype(bf16)
                right_hop(u, j).start()

    def relay_left(u):
        for j in range(replicas - 1):

            @pl.when(has_right & (rep > j))
            def _(j=j):
                left_hop(u, j).wait_recv()
                buf_l[u, j] = (mine(u, j) + buf_l[u, j].astype(f32)).astype(bf16)
                left_hop(u, j).start()

    near_left = rep * 2 < replicas

    def relay_near(u):
        @pl.when(near_left)
        def _():
            relay_right(u)

        @pl.when(jnp.logical_not(near_left))
        def _():
            relay_left(u)

    def relay_far(u):
        @pl.when(near_left)
        def _():
            relay_left(u)

        @pl.when(jnp.logical_not(near_left))
        def _():
            relay_right(u)

    def finish(u):
        c, h, a = 1 - u // 6, 1 - (u // 3) % 2, u % 3
        for j in range(replicas):

            @pl.when(rep == j)
            def _(j=j):
                total = mine(u, j)
                if j > 0:
                    right_hop(u, j).wait_recv()
                    total = total + buf_r[u, j].astype(f32)
                if j < replicas - 1:
                    left_hop(u, j).wait_recv()
                    total = total + buf_l[u, j].astype(f32)
                for i in range(3):
                    wout[h, c, a * 3 + i] = total[:, i * chans : (i + 1) * chans].astype(bf16)

    def advance(u):
        @pl.when((u >= LAG) & (u < 12 + LAG))
        def _():
            relay_near(u - LAG)

        @pl.when(u > LAG)
        def _():
            relay_far(u - LAG - 1)
            finish(u - LAG - 1)

    def group(g):
        def one(u, carry):
            unit(1 - g % 2, 1 - g // 2, u)
            lead(u)
            advance(u)
            return carry

        lax.fori_loop(3 * g, 3 * g + 3, one, 0)

    group(0)
    turn_all(0, 1)
    fetch_entries().wait()
    arrive_enc(final)
    upper(0, final, False)
    group(1)
    turn_all(1, 0)
    lower(1, final)
    fin[1] = outg[final, 1]
    group(2)
    turn_all(0, 0)
    lower(0, final)
    fin[0] = outg[final, 0]
    group(3)

    def rest(u, carry):
        advance(u)
        return carry

    lax.fori_loop(12, 13 + LAG, rest, 0)

    def drain(u, carry):
        for j in range(replicas):

            @pl.when(rep < j)
            def _(j=j):
                right_hop(u, j).wait_send()

            @pl.when(rep > j)
            def _(j=j):
                left_hop(u, j).wait_send()

        return carry

    lax.fori_loop(0, 12, drain, 0)

    def drain_chain(t, carry):
        @pl.when(has_up)
        def _():
            dec_hop(t).wait_send()

        @pl.when(has_down)
        def _():
            enc_hop(t).wait_send()

        return carry

    lax.fori_loop(0, ticks - 1, drain_chain, 0)


def on_device(pending, objective, entries, early, later, taps, slots):
    levels = lax.axis_size("section")
    replicas = lax.axis_size("dp")
    images, rows, cols, chans = pending.shape[2:]
    ticks = slots.shape[0]
    kept = entries.shape[2]
    pix = images * rows * cols
    scale = 1.0 / math.sqrt(ticks * replicas * pix)
    dims = (ticks, levels, replicas, rows, cols, chans)
    bf16 = jnp.bfloat16
    share = chans // replicas
    whole = pl.BlockSpec(memory_space=pltpu.VMEM)
    anywhere = pl.BlockSpec(memory_space=pl.ANY)
    dma = pltpu.SemaphoreType.DMA
    fin, wout = pl.pallas_call(
        functools.partial(kernel, dims),
        out_shape=(
            jax.ShapeDtypeStruct((2, pix, chans), bf16),
            jax.ShapeDtypeStruct((2, 2, 9, share, chans), bf16),
        ),
        in_specs=[pl.BlockSpec(memory_space=pltpu.SMEM)] + [whole] * 2 + [anywhere] * 4,
        out_specs=(whole, whole),
        scratch_shapes=[
            pltpu.VMEM((ticks - 1, pix, chans), bf16),
            pltpu.VMEM((2, kept, pix, chans), bf16),
            pltpu.VMEM((2, kept, pix, chans), bf16),
            pltpu.VMEM((2, 2, 9, chans, chans), bf16),
            dma((4, 2)),
            pltpu.VMEM((ticks, 2, pix, chans), bf16),
            pltpu.VMEM((ticks, 2, pix, chans), bf16),
            pltpu.VMEM((2, 2, ticks, 3, pix + 2 * cols, chans), bf16),
            pltpu.VMEM((2, 2, chans, ticks * pix), bf16),
            pltpu.VMEM((LAG + 2, chans, 3 * chans), jnp.float32),
            pltpu.VMEM((12, replicas, share, 3 * chans), bf16),
            pltpu.VMEM((12, replicas, share, 3 * chans), bf16),
            dma((ticks - 1,)),
            dma((ticks - 1,)),
            dma((ticks - 1,)),
            dma((ticks - 1,)),
            dma((12, replicas)),
            dma((12, replicas)),
            dma((12, replicas)),
            dma((12, replicas)),
        ],
        compiler_params=pltpu.CompilerParams(
            collective_id=0, has_side_effects=True, vmem_limit_bytes=67043328
        ),
    )(
        slots,
        pending.reshape(2, pix, chans),
        later.reshape(2, kept, pix, chans),
        objective.reshape(-1, pix, chans),
        early.reshape(2, kept, pix, chans),
        entries.reshape(2, kept, pix, chans),
        taps.reshape(2, 2, 9, chans, chans),
    )
    return (
        fin.reshape(2, 1, images, rows, cols, chans),
        (wout.astype(jnp.float32) * scale).reshape(2, 1, 2, 9, share, chans),
    )


def solution(mesh):
    placed = (
        P(None, "section", "dp", None, None, None),
        P(None, "dp", None, None, None),
        P(None, "section", None, "dp", None, None, None),
        P(None, "section", None, "dp", None, None, None),
        P(None, "section", None, "dp", None, None, None),
        P(None, "section", None, None, None, None),
        P(),
    )
    return jax.shard_map(
        on_device,
        mesh=mesh,
        in_specs=placed,
        out_specs=(
            P(None, "section", "dp", None, None, None),
            P(None, "section", None, None, "dp", None),
        ),
        check_vma=False,
    )
```
